32 devices in a mesh: section: 2 (over core), seq: 16 (over z, y, x).
Axes of the slice: x: 2, y: 2, z: 4, core: 2. Of those that a mesh axis runs over, the one named last changes fastest.
Arguments:
- queries: bfloat16 [4096, 4096], P('seq', 'section'), may hold values from -50 to 50
- key_rows: bfloat16 [4096, 4096], P('seq', 'section'), may hold values from -6 to 6
- value_rows: bfloat16 [4096, 4096], P('seq', 'section'), may hold values from -6 to 6
- block_pattern: int32 [32, 8], P('seq'), may hold values from 0 to 1, as said below
- out_weight: bfloat16 [4096, 4096], P('section'), may hold values from -0.09375 to 0.09375
- hidden: bfloat16 [4096, 4096], P('seq', 'section'), may hold values from -3 to 3
- norm_gain: float32 [4096], P('section'), may hold values from 0.5 to 1.5
Outputs:
- stream_out: bfloat16 [4096, 4096], P('seq', 'section')
- normed: bfloat16 [4096, 4096], P('seq', 'section')
The draws below stay inside these ranges and needn't reach their ends.
Inputs may be any that keep to these rules, and one draw needn't show every extreme that they name: `block_pattern`: column 0 is 1 in every row: every query block attends its own block.
All inputs are finite; a program needn't handle non-finite values.
Results may differ from the reference program's by a relative error of at most 0.008.
Values may be sent and summed in bfloat16 or wider, within the bound.
A program may use at most 128 MiB of HBM per device.

```python
import math
import jax
import jax.numpy as jnp
from jax import lax

D = 4096
HEADS = 32
HEAD_DIM = 128
BLOCK = 128
WINDOW_BLOCKS = 8
TOKENS = 4096
NBLK = 32
N_SECTION = 2


def joint_draw(key):
    full_shape = (TOKENS, D)
    query_key = jax.random.fold_in(key, 101)
    keys_key = jax.random.fold_in(key, 202)
    query_draw = jnp.clip(2.0 * jax.random.normal(query_key, full_shape, jnp.float32), -12.0, 12.0)
    key_draw = jnp.clip(jax.random.normal(keys_key, full_shape, jnp.float32), -6.0, 6.0)
    return (query_draw, key_draw)


def draw_queries(key, part):
    query_draw, key_draw = joint_draw(key)
    return query_draw.astype(jnp.bfloat16)


def draw_key_rows(key, part):
    query_draw, key_draw = joint_draw(key)
    return key_draw.astype(jnp.bfloat16)


def draw_block_pattern(key, part):
    picked = jax.random.randint(jax.random.fold_in(key, 303), (NBLK, WINDOW_BLOCKS), 0, 2, jnp.int32)
    column = jnp.arange(WINDOW_BLOCKS, dtype=jnp.int32)[None, :]
    return jnp.where(column == 0, 1, picked).astype(jnp.int32)


def draw_hidden(key, part):
    column_scale = 0.5 + jnp.arange(D, dtype=jnp.float32) / D
    base_key = jax.random.fold_in(key, 404)
    noise = jnp.clip(jax.random.normal(base_key, (TOKENS, D), jnp.float32), -6.0, 6.0)
    values = 0.3 * noise * column_scale[None, :]
    return values.astype(jnp.bfloat16)


def block_levels(rng, extent, shards, low, top_value):
    def one(dim, blocks):
        draws = jax.random.uniform(jax.random.fold_in(jax.random.fold_in(rng, 6), dim), (blocks,), jnp.float32, low / len(shards), top_value / len(shards))
        return jnp.repeat(jnp.exp(draws), extent[dim] // blocks).reshape((-1,) + (1,) * (len(extent) - dim - 1))

    level = one(*shards[0])
    for cut in shards[1:]:
        level = level * one(*cut)
    return level


def gaussian(key, dims, deviation, bound, pieces=(), kind=jnp.bfloat16):
    values = deviation * jax.random.normal(key, dims, jnp.float32)
    if pieces:
        values = values * block_levels(key, dims, pieces, -0.22, 0.18)
    return jnp.clip(values, -bound, bound).astype(kind)


def setup_inputs(seed: int = 0) -> dict:
    keys = jax.random.split(jax.random.key(seed), 8)
    return {
        "queries": draw_queries(jax.random.fold_in(keys[7], 71), 0),
        "key_rows": draw_key_rows(jax.random.fold_in(keys[7], 71), 0),
        "value_rows": gaussian(keys[2], (TOKENS, D), 1.0, 6.0, ((0, 16), (1, 2))),
        "block_pattern": draw_block_pattern(jax.random.fold_in(keys[7], 71), 0),
        "out_weight": gaussian(keys[4], (D, D), D ** -0.5, 0.09375, ((0, 2),)),
        "hidden": draw_hidden(jax.random.fold_in(keys[7], 71), 0),
        "norm_gain": jnp.clip(1.0 + 0.1 * jax.random.normal(keys[6], (D,), jnp.float32), 0.5, 1.5),
    }


def window_attention(queries, key_rows, value_rows, block_pattern):
    token_count = queries.shape[0]
    block_count = token_count // BLOCK
    front_rows = (WINDOW_BLOCKS - 1) * BLOCK
    padded_keys = jnp.concatenate([jnp.zeros((front_rows, D), key_rows.dtype), key_rows], 0)
    padded_values = jnp.concatenate([jnp.zeros((front_rows, D), value_rows.dtype), value_rows], 0)
    window_span = WINDOW_BLOCKS * BLOCK
    offsets = (WINDOW_BLOCKS - 1 - jnp.arange(window_span, dtype=jnp.int32) // BLOCK).astype(jnp.int32)
    key_place = jnp.arange(window_span, dtype=jnp.int32) % BLOCK
    query_place = jnp.arange(BLOCK, dtype=jnp.int32)
    scaling = 1.0 / math.sqrt(HEAD_DIM)

    def one_block(block_index):
        begin_row = (block_index * BLOCK).astype(jnp.int32)
        query_block = lax.dynamic_slice_in_dim(queries, begin_row, BLOCK, 0).astype(jnp.float32).reshape(BLOCK, HEADS, HEAD_DIM)
        key_block = lax.dynamic_slice_in_dim(padded_keys, begin_row, window_span, 0).astype(jnp.float32).reshape(window_span, HEADS, HEAD_DIM)
        value_block = lax.dynamic_slice_in_dim(padded_values, begin_row, window_span, 0).astype(jnp.float32).reshape(window_span, HEADS, HEAD_DIM)
        pattern_row = lax.dynamic_index_in_dim(block_pattern, block_index, 0, keepdims=False)
        allowed = (pattern_row[offsets] == 1) & (block_index - offsets >= 0)
        causal = (offsets[None, :] > 0) | (key_place[None, :] <= query_place[:, None])
        visible = allowed[None, :] & causal
        scores = jnp.einsum('qhd,khd->hqk', query_block, key_block) * scaling
        scores = jnp.where(visible[None], scores, -jnp.inf)
        largest = lax.optimization_barrier(jnp.max(scores, axis=2, keepdims=True))
        exponent = jnp.exp(scores - largest)
        weights = (exponent / lax.optimization_barrier(jnp.sum(exponent, axis=2, keepdims=True))).astype(jnp.bfloat16)
        mixture = jnp.einsum('hqk,khd->qhd', weights.astype(jnp.float32), value_block)
        return mixture.reshape(BLOCK, D).astype(jnp.bfloat16)
    result = lax.map(one_block, jnp.arange(block_count, dtype=jnp.int32))
    return result.reshape(token_count, D)

def reference(queries, key_rows, value_rows, block_pattern, out_weight, hidden, norm_gain):
    attended = window_attention(queries, key_rows, value_rows, block_pattern)
    group_width = D // N_SECTION
    projected = jnp.zeros((TOKENS, D), jnp.float32)
    for group_index in range(N_SECTION):
        low = group_index * group_width
        group_part = jnp.dot(attended[:, low:low + group_width], out_weight[low:low + group_width], preferred_element_type=jnp.float32).astype(jnp.bfloat16)
        projected = projected + lax.optimization_barrier(group_part).astype(jnp.float32)
    stream = hidden.astype(jnp.float32) + projected
    mean_square = lax.optimization_barrier(jnp.mean(stream * stream, axis=1, keepdims=True))
    normed = stream * lax.rsqrt(mean_square + 1e-06) * norm_gain[None, :]
    return (stream.astype(jnp.bfloat16), normed.astype(jnp.bfloat16))
```

```python
import functools
import math

import jax
import jax.numpy as jnp
from jax import lax
from jax.experimental import pallas as pl
from jax.experimental.pallas import tpu as pltpu
from jax.sharding import PartitionSpec as P

HEAD_DIM = 128
BLOCK = 128
WINDOW_BLOCKS = 8
GROUP = 4
FAR = 5
MESH = pl.DeviceIdType.MESH
HIDE = -1e30


def kernel(
    q_hbm, k_hbm, v_hbm, pattern, w_hbm, h_hbm, gain,
    stream_ref, normed_ref,
    kv, qbuf, wbuf, hbuf, bias, acc, mixed, outgoing, incoming, square_out, square_in,
    own_sem, load_sem, send_sem, recv_sem, part_send, part_recv, sq_sem,
):
    rows, width = q_hbm.shape
    model = w_hbm.shape[1]
    subs = own_sem.shape[1]
    step_cols = width // subs
    piece = step_cols // 2
    shard = lax.axis_index("seq")
    section = lax.axis_index("section")
    count = lax.axis_size("seq")
    role = lax.rem(shard, GROUP)
    has_prev = shard >= GROUP
    has_next = shard + GROUP < count
    partner = 1 - section

    def base(off):
        return (FAR - off) * rows

    def view(off, k, part, tail):
        start = k * step_cols + (piece if part == 1 else 0)
        size = step_cols if part is None else piece
        cols = pl.ds(pl.multiple_of(start, piece), size)
        first, extent = (base(off) + rows - BLOCK, BLOCK) if tail else (base(off), rows)
        return kv.at[:, pl.ds(first, extent), cols]

    def part_index(part):
        return 1 if part == 1 else 0

    def send(index, k, off, target, to_off, part=None, tail=False):
        return pltpu.make_async_remote_copy(
            src_ref=view(off, k, part, tail),
            dst_ref=view(to_off, k, part, tail),
            send_sem=send_sem.at[index, k],
            recv_sem=recv_sem.at[to_off + 1, part_index(part), k],
            device_id={"seq": target},
            device_id_type=MESH,
        )

    def arrive(k, off, part=None, tail=False):
        pltpu.make_async_remote_copy(
            src_ref=view(off, k, part, tail),
            dst_ref=view(off, k, part, tail),
            send_sem=send_sem.at[0, k],
            recv_sem=recv_sem.at[off + 1, part_index(part), k],
            device_id={"section": partner},
            device_id_type=MESH,
        ).wait_recv()

    def own_loads(k):
        cols = pl.ds(pl.multiple_of(k * step_cols, step_cols), step_cols)
        return [
            pltpu.make_async_copy(
                source.at[:, cols], kv.at[i, pl.ds(base(0), rows), cols], own_sem.at[i, k]
            )
            for i, source in enumerate((k_hbm, v_hbm))
        ]

    a_own = [
        (0, 0, 1, 1, None, False, None),
        (1, 0, 2, 2, None, False, None),
        (2, 0, 4, 4, None, True, "next"),
    ]
    a_first = [(3, -1, 2, 1, 0, False, None), (4, -1, 4, 3, 0, False, "next")]
    a_second = [(5, 2, 1, 3, 0, False, "prev")]
    b_own = [
        (0, 0, -1, -1, 0, False, None),
        (1, 0, 2, 2, None, False, None),
        (2, 0, 4, 4, 1, False, "next"),
        (3, 0, 4, 4, 0, True, "next"),
    ]
    b_first = [(4, 1, 2, 3, 0, False, None), (5, 4, -1, 3, 1, False, "prev")]
    b_second = [(6, 2, -1, 1, 0, False, "prev")]
    c_own = [(0, 0, 1, 1, None, False, None), (1, 0, 4, 4, None, False, "next")]
    c_first = [(2, 2, 1, 3, 1, False, None), (3, 4, -2, 2, None, False, "prev")]
    c_second = [(4, 3, -2, 1, 1, False, "prev")]
    d_own = [(0, 0, 4, 4, None, False, "next")]
    d_first = [
        (1, 4, -2, 2, None, False, "prev"),
        (2, 4, -1, 3, None, False, "prev"),
        (3, 2, -1, 1, 1, False, None),
        (4, 1, 4, 5, 1, False, "next"),
    ]
    d_second = [(5, 5, -2, 3, 1, False, "prev")]
    table = [
        (a_own, [(-1, 0, False, None)], a_first,
         [(2, None, False, "prev")], a_second,
         [(1, 0, False, "prev"), (1, 1, False, "prev"), (3, 0, False, "prev"),
          (3, 1, False, "prev"), (4, None, True, "prev")]),
        (b_own, [(1, None, False, None), (4, 1, False, "prev")], b_first,
         [(2, None, False, "prev")], b_second,
         [(3, 0, False, "prev"), (3, 1, False, "prev"), (4, 0, True, "prev")]),
        (c_own, [(2, None, False, None), (4, None, False, "prev")], c_first,
         [(3, None, False, "prev")], c_second,
         [(1, 0, False, None), (1, 1, False, None)]),
        (d_own, [(4, None, False, "prev"), (2, None, False, None), (1, None, False, None)], d_first,
         [(5, 1, False, "prev")], d_second,
         [(3, 0, False, None), (3, 1, False, None)]),
    ]

    def grouped(entries, act):
        for need in (None, "prev", "next"):
            chosen = [e for e in entries if e[-1] == need]
            if not chosen:
                continue
            if need is None:
                for e in chosen:
                    act(e)
            else:
                @pl.when(has_prev if need == "prev" else has_next)
                def _():
                    for e in chosen:
                        act(e)

    def start_sends(entries, k):
        def act(e):
            index, off, step, to_off, part, tail, _ = e
            send(index, k, off, shard + step, to_off, part, tail).start()

        grouped(entries, act)

    def end_sends(entries, k):
        def act(e):
            index, off, step, to_off, part, tail, _ = e
            send(index, k, off, shard + step, to_off, part, tail).wait_send()

        grouped(entries, act)

    def waits(entries, k):
        grouped(entries, lambda e: arrive(k, e[0], e[1], e[2]))

    def by_role(body):
        for r in range(GROUP):
            @pl.when(role == r)
            def _():
                body(table[r])

    def first_sends(k):
        for copy in own_loads(k):
            copy.wait()
        by_role(lambda row: start_sends(row[0], k))

    def first_relay(k):
        def body(row):
            waits(row[1], k)
            start_sends(row[2], k)

        by_role(body)

    def second_relay(k):
        def body(row):
            waits(row[3], k)
            start_sends(row[4], k)

        by_role(body)

    q_load = pltpu.make_async_copy(q_hbm, qbuf, load_sem.at[0])
    w_load = pltpu.make_async_copy(w_hbm, wbuf, load_sem.at[1])
    h_load = pltpu.make_async_copy(h_hbm, hbuf, load_sem.at[2])

    for k in range(subs):
        for copy in own_loads(k):
            copy.start()
    q_load.start()
    w_load.start()
    h_load.start()

    barrier = pltpu.get_barrier_semaphore()
    across = jnp.where(lax.rem(role, 2) == 0, shard + 1, shard - 1)
    along = jnp.where(role < 2, shard + 2, shard - 2)
    pl.semaphore_signal(barrier, inc=1, device_id={"seq": across}, device_id_type=MESH)
    pl.semaphore_signal(barrier, inc=1, device_id={"seq": along}, device_id_type=MESH)
    pl.semaphore_signal(barrier, inc=1, device_id={"section": partner}, device_id_type=MESH)

    @pl.when(has_prev)
    def _():
        pl.semaphore_signal(
            barrier, inc=1, device_id={"seq": shard - GROUP}, device_id_type=MESH
        )

    @pl.when(has_next)
    def _():
        pl.semaphore_signal(
            barrier, inc=1, device_id={"seq": shard + GROUP}, device_id_type=MESH
        )

    pl.semaphore_wait(barrier, 3 + has_prev.astype(jnp.int32) + has_next.astype(jnp.int32))

    first_sends(0)

    for off in range(1, GROUP + 1):
        @pl.when(shard < off)
        def _():
            kv[:, pl.ds(base(off), rows), :] = jnp.zeros((2, rows, width), kv.dtype)

    query_place = lax.broadcasted_iota(jnp.int32, (BLOCK, BLOCK), 0)
    key_place = lax.broadcasted_iota(jnp.int32, (BLOCK, BLOCK), 1)
    blocks = rows // BLOCK
    span_blocks = WINDOW_BLOCKS - 1 + blocks
    for i in range(blocks):
        for g in range(span_blocks):
            j = i + WINDOW_BLOCKS - 1 - g
            if j < 0 or j >= WINDOW_BLOCKS:
                value = jnp.full((BLOCK, BLOCK), HIDE, jnp.float32)
            else:
                seen = (pattern[i, j] == 1) & (shard * blocks + i - j >= 0)
                level = jnp.where(seen, 0.0, HIDE).astype(jnp.float32)
                value = jnp.full((BLOCK, BLOCK), level, jnp.float32)
                if j == 0:
                    value = jnp.where(key_place <= query_place, value, HIDE)
            bias[i * BLOCK : (i + 1) * BLOCK, g * BLOCK : (g + 1) * BLOCK] = value
    acc[...] = jnp.zeros(acc.shape, acc.dtype)
    q_load.wait()
    w_load.wait()
    h_load.wait()

    key_first = base(GROUP) + rows - BLOCK
    key_span = span_blocks * BLOCK
    factor = math.log2(math.e) / math.sqrt(HEAD_DIM)
    tile = math.gcd(model, 1024)

    def attend(k):
        by_role(lambda row: waits(row[5], k))
        for n in range(step_cols // HEAD_DIM):
            cols = pl.ds(pl.multiple_of(k * step_cols + n * HEAD_DIM, HEAD_DIM), HEAD_DIM)
            query = qbuf[:, cols]
            keys = kv[0, pl.ds(key_first, key_span), cols]
            values = kv[1, pl.ds(key_first, key_span), cols]
            scores = lax.dot_general(
                query, keys, (((1,), (1,)), ((), ())), preferred_element_type=jnp.float32
            )
            scores = scores + bias[...]
            largest = jnp.max(scores, axis=1, keepdims=True)
            exponent = jnp.exp2((scores - largest) * factor)
            total = jnp.sum(exponent, axis=1, keepdims=True)
            mixture = jnp.dot(
                exponent.astype(jnp.bfloat16), values, preferred_element_type=jnp.float32
            )
            mixed[:, n * HEAD_DIM : (n + 1) * HEAD_DIM] = (mixture / total).astype(jnp.bfloat16)
        depth = pl.ds(pl.multiple_of(k * step_cols, step_cols), step_cols)
        for c in range(0, model, tile):
            acc[:, c : c + tile] += jnp.dot(
                mixed[...], wbuf[depth, c : c + tile], preferred_element_type=jnp.float32
            )

    @pl.loop(0, subs + 2)
    def _(t):
        @pl.when(t + 1 < subs)
        def _():
            first_sends(t + 1)

        @pl.when(t < subs)
        def _():
            first_relay(t)

        @pl.when((t >= 1) & (t - 1 < subs))
        def _():
            second_relay(t - 1)

        @pl.when(t >= 2)
        def _():
            attend(t - 2)

    pieces = part_send.shape[0]
    part_cols = width // pieces

    def part_copy(c):
        cols = pl.ds(c * part_cols, part_cols)
        return pltpu.make_async_remote_copy(
            src_ref=outgoing.at[:, cols],
            dst_ref=incoming.at[:, cols],
            send_sem=part_send.at[c],
            recv_sem=part_recv.at[c],
            device_id={"section": partner},
            device_id_type=MESH,
        )

    for c in range(pieces):
        start = pl.multiple_of(partner * width + c * part_cols, part_cols)
        outgoing[:, c * part_cols : (c + 1) * part_cols] = acc[:, pl.ds(start, part_cols)].astype(
            outgoing.dtype
        )
        if c >= 1:
            part_copy(c - 1).start()
    part_copy(pieces - 1).start()

    @pl.loop(0, subs)
    def _(k):
        def body(row):
            for entries in (row[0], row[2], row[4]):
                end_sends(entries, k)

        by_role(body)

    strip = 16
    mine = pl.multiple_of(section * width, part_cols)
    for c in range(pieces):
        part_copy(c).wait_recv()

    @pl.loop(0, rows // strip)
    def _(i):
        place = pl.ds(pl.multiple_of(i * strip, strip), strip)
        here = acc[place, pl.ds(mine, width)].astype(jnp.bfloat16).astype(jnp.float32)
        there = incoming[place, :].astype(jnp.float32)
        stream = hbuf[place, :].astype(jnp.float32) + (here + there)
        acc[place, pl.ds(mine, width)] = stream
        stream_ref[place, :] = stream.astype(stream_ref.dtype)
        squares = stream * stream
        lanes = squares[:, 0:128]
        for c in range(128, width, 128):
            lanes = lanes + squares[:, c : c + 128]
        square_out[place, :] = lanes

    square_copy = pltpu.make_async_remote_copy(
        src_ref=square_out,
        dst_ref=square_in,
        send_sem=sq_sem.at[0],
        recv_sem=sq_sem.at[1],
        device_id={"section": partner},
        device_id_type=MESH,
    )
    square_copy.start()
    for c in range(pieces):
        part_copy(c).wait_send()
    square_copy.wait()

    @pl.loop(0, rows // strip)
    def _(i):
        place = pl.ds(pl.multiple_of(i * strip, strip), strip)
        squares = jnp.sum(square_out[place, :] + square_in[place, :], axis=1, keepdims=True)
        inverse = lax.rsqrt(squares / model + 1e-06)
        stream = acc[place, pl.ds(mine, width)]
        normed_ref[place, :] = (stream * inverse * gain[...]).astype(normed_ref.dtype)


def shards(queries, key_rows, value_rows, block_pattern, out_weight, hidden, norm_gain):
    rows, width = queries.shape
    model = out_weight.shape[1]
    subs = width // (2 * HEAD_DIM)
    pieces = 4
    span = (WINDOW_BLOCKS - 1) * BLOCK + rows
    anywhere = pl.BlockSpec(memory_space=pl.ANY)
    vmem = pl.BlockSpec(memory_space=pltpu.VMEM)
    out = jax.ShapeDtypeStruct((rows, width), jnp.bfloat16)
    return pl.pallas_call(
        kernel,
        out_shape=(out, out),
        in_specs=[
            anywhere, anywhere, anywhere,
            pl.BlockSpec(memory_space=pltpu.SMEM),
            anywhere, anywhere, vmem,
        ],
        out_specs=(vmem, vmem),
        scratch_shapes=[
            pltpu.VMEM((2, (FAR + 2) * rows, width), jnp.bfloat16),
            pltpu.VMEM((rows, width), jnp.bfloat16),
            pltpu.VMEM((width, model), jnp.bfloat16),
            pltpu.VMEM((rows, width), jnp.bfloat16),
            pltpu.VMEM((rows, span), jnp.float32),
            pltpu.VMEM((rows, model), jnp.float32),
            pltpu.VMEM((rows, 2 * HEAD_DIM), jnp.bfloat16),
            pltpu.VMEM((rows, width), jnp.bfloat16),
            pltpu.VMEM((rows, width), jnp.bfloat16),
            pltpu.VMEM((rows, 128), jnp.float32),
            pltpu.VMEM((rows, 128), jnp.float32),
            pltpu.SemaphoreType.DMA((2, subs)),
            pltpu.SemaphoreType.DMA((3,)),
            pltpu.SemaphoreType.DMA((7, subs)),
            pltpu.SemaphoreType.DMA((FAR + 2, 2, subs)),
            pltpu.SemaphoreType.DMA((pieces,)),
            pltpu.SemaphoreType.DMA((pieces,)),
            pltpu.SemaphoreType.DMA((2,)),
        ],
        compiler_params=pltpu.CompilerParams(
            collective_id=0, has_side_effects=True, vmem_limit_bytes=62 * 1024 * 1024
        ),
    )(queries, key_rows, value_rows, block_pattern, out_weight, hidden, norm_gain[None, :])


def solution(mesh):
    placed = (
        P("seq", "section"),
        P("seq", "section"),
        P("seq", "section"),
        P("seq", None),
        P("section", None),
        P("seq", "section"),
        P("section"),
    )
    return jax.shard_map(
        shards,
        mesh=mesh,
        in_specs=placed,
        out_specs=(P("seq", "section"), P("seq", "section")),
        check_vma=False,
    )
```

```python
import functools
import math

import jax
import jax.numpy as jnp
from jax import lax
from jax.experimental import pallas as pl
from jax.experimental.pallas import tpu as pltpu
from jax.sharding import PartitionSpec as P

HEAD_DIM = 128
BLOCK = 128
WINDOW_BLOCKS = 8
GROUP = 4
FAR = 5
MESH = pl.DeviceIdType.MESH
HIDE = -1e30


def kernel(
    q_hbm, k_hbm, v_hbm, pattern, w_hbm, h_hbm,
    stream_ref, square_ref,
    kv, qbuf, wbuf, hbuf, bias, acc, mixed, mine, outgoing, incoming, square_out, square_in,
    own_sem, load_sem, send_sem, recv_sem, part_send, part_recv, sq_sem,
):
    rows, width = q_hbm.shape
    model = w_hbm.shape[1]
    subs = own_sem.shape[1]
    step_cols = width // subs
    piece = step_cols // 2
    shard = lax.axis_index("seq")
    section = lax.axis_index("section")
    count = lax.axis_size("seq")
    role = lax.rem(shard, GROUP)
    has_prev = shard >= GROUP
    has_next = shard + GROUP < count
    partner = 1 - section

    def base(off):
        return (FAR - off) * rows

    def view(off, k, part, tail):
        start = k * step_cols + (piece if part == 1 else 0)
        size = step_cols if part is None else piece
        cols = pl.ds(pl.multiple_of(start, piece), size)
        first, extent = (base(off) + rows - BLOCK, BLOCK) if tail else (base(off), rows)
        return kv.at[:, pl.ds(first, extent), cols]

    def part_index(part):
        return 1 if part == 1 else 0

    def send(index, k, off, target, to_off, part=None, tail=False):
        return pltpu.make_async_remote_copy(
            src_ref=view(off, k, part, tail),
            dst_ref=view(to_off, k, part, tail),
            send_sem=send_sem.at[index, k],
            recv_sem=recv_sem.at[to_off + 1, part_index(part), k],
            device_id={"seq": target},
            device_id_type=MESH,
        )

    def arrive(k, off, part=None, tail=False):
        pltpu.make_async_remote_copy(
            src_ref=view(off, k, part, tail),
            dst_ref=view(off, k, part, tail),
            send_sem=send_sem.at[0, k],
            recv_sem=recv_sem.at[off + 1, part_index(part), k],
            device_id={"section": partner},
            device_id_type=MESH,
        ).wait_recv()

    def own_loads(k):
        cols = pl.ds(pl.multiple_of(k * step_cols, step_cols), step_cols)
        return [
            pltpu.make_async_copy(
                source.at[:, cols], kv.at[i, pl.ds(base(0), rows), cols], own_sem.at[i, k]
            )
            for i, source in enumerate((k_hbm, v_hbm))
        ]

    table = [
        (
            [(0, 0, 1, 1, 0, False, None), (1, 0, 2, 2, 0, False, None),
             (2, 0, 1, 1, 1, False, None), (3, 0, 2, 2, 1, False, None),
             (4, 0, 4, 4, None, True, "next")],
            [([(-1, 0, False, None)],
              [(5, -1, 2, 1, 0, False, None), (6, -1, 4, 3, 0, False, "next")])],
            [([(2, 0, False, "prev")], [(7, 2, 1, 3, 0, False, "prev")])],
            [(2, 1, False, "prev"), (3, 0, False, "prev"), (4, None, True, "prev"),
             (3, 1, False, "prev"), (1, 0, False, "prev"), (1, 1, False, "prev")],
        ),
        (
            [(0, 0, -1, -1, 0, False, None), (1, 0, 2, 2, 1, False, None),
             (2, 0, 4, 4, 1, False, "next"), (3, 0, 2, 2, 0, False, None),
             (4, 0, 4, 4, 0, True, "next")],
            [([(4, 1, False, "prev")], [(5, 4, -1, 3, 1, False, "prev")]),
             ([(1, 0, False, None)], [(6, 1, 2, 3, 0, False, None)])],
            [([(2, 0, False, "prev")], [(7, 2, -1, 1, 0, False, "prev")])],
            [(1, 1, False, None), (2, 1, False, "prev"), (4, 0, True, "prev"),
             (3, 0, False, "prev"), (3, 1, False, "prev")],
        ),
        (
            [(0, 0, 4, 4, 0, False, "next"), (1, 0, 1, 1, 1, False, None),
             (2, 0, 4, 4, 1, False, "next"), (3, 0, 1, 1, 0, False, None)],
            [([(4, 0, False, "prev")], [(4, 4, -2, 2, 0, False, "prev")]),
             ([(4, 1, False, "prev")], [(5, 4, -2, 2, 1, False, "prev")]),
             ([(2, 1, False, None)], [(6, 2, 1, 3, 1, False, None)])],
            [([(3, 1, False, "prev")], [(7, 3, -2, 1, 1, False, "prev")])],
            [(2, 0, False, None), (3, 0, False, "prev"),
             (1, 0, False, None), (1, 1, False, None)],
        ),
        (
            [(0, 0, 4, 4, 0, False, "next"), (1, 0, 4, 4, 1, False, "next")],
            [([(4, 0, False, "prev")],
              [(2, 4, -2, 2, 0, False, "prev"), (3, 4, -1, 3, 0, False, "prev")]),
             ([(4, 1, False, "prev")],
              [(4, 4, -1, 3, 1, False, "prev"), (5, 4, -2, 2, 1, False, "prev")]),
             ([(2, 1, False, None)], [(6, 2, -1, 1, 1, False, None)]),
             ([(1, 1, False, None)], [(7, 1, 4, 5, 1, False, "next")])],
            [([(5, 1, False, "prev")], [(8, 5, -2, 3, 1, False, "prev")])],
            [(2, 0, False, None), (1, 0, False, None),
             (3, 0, False, None), (3, 1, False, None)],
        ),
    ]

    def grouped(entries, act):
        for need in (None, "prev", "next"):
            chosen = [e for e in entries if e[-1] == need]
            if not chosen:
                continue
            if need is None:
                for e in chosen:
                    act(e)
            else:
                @pl.when(has_prev if need == "prev" else has_next)
                def _():
                    for e in chosen:
                        act(e)

    def start_sends(entries, k):
        def act(e):
            index, off, step, to_off, part, tail, _ = e
            send(index, k, off, shard + step, to_off, part, tail).start()

        grouped(entries, act)

    def end_sends(entries, k):
        def act(e):
            index, off, step, to_off, part, tail, _ = e
            send(index, k, off, shard + step, to_off, part, tail).wait_send()

        grouped(entries, act)

    def waits(entries, k):
        grouped(entries, lambda e: arrive(k, e[0], e[1], e[2]))

    def by_role(body):
        for r in range(GROUP):
            @pl.when(role == r)
            def _():
                body(table[r])

    def first_sends(k):
        for copy in own_loads(k):
            copy.wait()
        by_role(lambda row: start_sends(row[0], k))

    def relay(which, k):
        def body(row):
            for needed, sends in row[which]:
                waits(needed, k)
                start_sends(sends, k)

        by_role(body)

    q_load = pltpu.make_async_copy(q_hbm, qbuf, load_sem.at[0])
    w_load = pltpu.make_async_copy(w_hbm, wbuf, load_sem.at[1])
    h_load = pltpu.make_async_copy(h_hbm, hbuf, load_sem.at[2])

    for k in range(subs):
        for copy in own_loads(k):
            copy.start()
    q_load.start()
    w_load.start()
    h_load.start()

    barrier = pltpu.get_barrier_semaphore()
    across = jnp.where(lax.rem(role, 2) == 0, shard + 1, shard - 1)
    along = jnp.where(role < 2, shard + 2, shard - 2)
    pl.semaphore_signal(barrier, inc=1, device_id={"seq": across}, device_id_type=MESH)
    pl.semaphore_signal(barrier, inc=1, device_id={"seq": along}, device_id_type=MESH)
    pl.semaphore_signal(barrier, inc=1, device_id={"section": partner}, device_id_type=MESH)

    @pl.when(has_prev)
    def _():
        pl.semaphore_signal(
            barrier, inc=1, device_id={"seq": shard - GROUP}, device_id_type=MESH
        )

    @pl.when(has_next)
    def _():
        pl.semaphore_signal(
            barrier, inc=1, device_id={"seq": shard + GROUP}, device_id_type=MESH
        )

    pl.semaphore_wait(barrier, 3 + has_prev.astype(jnp.int32) + has_next.astype(jnp.int32))

    first_sends(0)

    for off in range(1, GROUP + 1):
        @pl.when(shard < off)
        def _():
            kv[:, pl.ds(base(off), rows), :] = jnp.zeros((2, rows, width), kv.dtype)

    query_place = lax.broadcasted_iota(jnp.int32, (BLOCK, BLOCK), 0)
    key_place = lax.broadcasted_iota(jnp.int32, (BLOCK, BLOCK), 1)
    blocks = rows // BLOCK
    span_blocks = WINDOW_BLOCKS - 1 + blocks
    for i in range(blocks):
        for g in range(span_blocks):
            j = i + WINDOW_BLOCKS - 1 - g
            if j < 0 or j >= WINDOW_BLOCKS:
                value = jnp.full((BLOCK, BLOCK), HIDE, jnp.float32)
            else:
                seen = (pattern[i, j] == 1) & (shard * blocks + i - j >= 0)
                level = jnp.where(seen, 0.0, HIDE).astype(jnp.float32)
                value = jnp.full((BLOCK, BLOCK), level, jnp.float32)
                if j == 0:
                    value = jnp.where(key_place <= query_place, value, HIDE)
            bias[i * BLOCK : (i + 1) * BLOCK, g * BLOCK : (g + 1) * BLOCK] = value
    acc[...] = jnp.zeros(acc.shape, acc.dtype)
    q_load.wait()
    w_load.wait()
    h_load.wait()

    key_first = base(GROUP) + rows - BLOCK
    key_span = span_blocks * BLOCK
    factor = math.log2(math.e) / math.sqrt(HEAD_DIM)
    tile = math.gcd(model, 1024)

    def heads(k):
        by_role(lambda row: waits(row[3], k))
        for n in range(step_cols // HEAD_DIM):
            cols = pl.ds(pl.multiple_of(k * step_cols + n * HEAD_DIM, HEAD_DIM), HEAD_DIM)
            query = qbuf[:, cols]
            keys = kv[0, pl.ds(key_first, key_span), cols]
            values = kv[1, pl.ds(key_first, key_span), cols]
            scores = lax.dot_general(
                query, keys, (((1,), (1,)), ((), ())), preferred_element_type=jnp.float32
            )
            scores = scores + bias[...]
            largest = jnp.max(scores, axis=1, keepdims=True)
            exponent = jnp.exp2((scores - largest) * factor)
            total = jnp.sum(exponent, axis=1, keepdims=True)
            mixture = jnp.dot(
                exponent.astype(jnp.bfloat16), values, preferred_element_type=jnp.float32
            )
            mixed[:, n * HEAD_DIM : (n + 1) * HEAD_DIM] = (mixture / total).astype(jnp.bfloat16)

    def attend(k):
        heads(k)
        depth = pl.ds(pl.multiple_of(k * step_cols, step_cols), step_cols)
        for c in range(0, model, tile):
            acc[:, c : c + tile] += jnp.dot(
                mixed[...], wbuf[depth, c : c + tile], preferred_element_type=jnp.float32
            )

    @pl.loop(0, subs)
    def _(t):
        @pl.when(t + 1 < subs)
        def _():
            first_sends(t + 1)

        relay(1, t)

        @pl.when(t >= 1)
        def _():
            relay(2, t - 1)

        @pl.when(t >= 2)
        def _():
            attend(t - 2)

    attend(subs - 2)
    relay(2, subs - 1)
    heads(subs - 1)

    pieces = part_send.shape[0]
    part_cols = width // pieces

    def part_copy(c):
        cols = pl.ds(c * part_cols, part_cols)
        return pltpu.make_async_remote_copy(
            src_ref=outgoing.at[:, cols],
            dst_ref=incoming.at[:, cols],
            send_sem=part_send.at[c],
            recv_sem=part_recv.at[c],
            device_id={"section": partner},
            device_id_type=MESH,
        )

    last = pl.ds((subs - 1) * step_cols, step_cols)

    def last_sum(start):
        cols = pl.ds(pl.multiple_of(start, part_cols), part_cols)
        return acc[:, cols] + jnp.dot(
            mixed[...], wbuf[last, cols], preferred_element_type=jnp.float32
        )

    for c in range(pieces):
        outgoing[:, c * part_cols : (c + 1) * part_cols] = last_sum(
            partner * width + c * part_cols
        ).astype(outgoing.dtype)
        if c >= 1:
            part_copy(c - 1).start()
    for c in range(pieces):
        cols = slice(c * part_cols, (c + 1) * part_cols)
        mine[:, cols] = last_sum(section * width + c * part_cols).astype(mine.dtype)
        if c == 0:
            part_copy(pieces - 1).start()
    for c in range(pieces):
        part_copy(c).wait_recv()

    strip = 16

    @pl.loop(0, rows // strip)
    def _(i):
        place = pl.ds(pl.multiple_of(i * strip, strip), strip)
        here = mine[place, :].astype(jnp.float32)
        there = incoming[place, :].astype(jnp.float32)
        stream = hbuf[place, :].astype(jnp.float32) + (here + there)
        stream_ref[place, :] = stream
        squares = stream * stream
        lanes = squares[:, 0:128]
        for c in range(128, width, 128):
            lanes = lanes + squares[:, c : c + 128]
        square_out[place, :] = lanes

    square_copy = pltpu.make_async_remote_copy(
        src_ref=square_out,
        dst_ref=square_in,
        send_sem=sq_sem.at[0],
        recv_sem=sq_sem.at[1],
        device_id={"section": partner},
        device_id_type=MESH,
    )
    square_copy.start()

    @pl.loop(0, subs)
    def _(k):
        def body(row):
            end_sends(row[0], k)
            for which in (1, 2):
                for _, sends in row[which]:
                    end_sends(sends, k)

        by_role(body)

    for c in range(pieces):
        part_copy(c).wait_send()
    square_copy.wait()
    square_ref[...] = square_out[...] + square_in[...]


def shards(queries, key_rows, value_rows, block_pattern, out_weight, hidden, norm_gain):
    rows, width = queries.shape
    model = out_weight.shape[1]
    subs = width // (2 * HEAD_DIM)
    pieces = 4
    span = (WINDOW_BLOCKS - 1) * BLOCK + rows
    anywhere = pl.BlockSpec(memory_space=pl.ANY)
    vmem = pl.BlockSpec(memory_space=pltpu.VMEM)
    stream, squares = pl.pallas_call(
        kernel,
        out_shape=(
            jax.ShapeDtypeStruct((rows, width), jnp.float32),
            jax.ShapeDtypeStruct((rows, 128), jnp.float32),
        ),
        in_specs=[
            anywhere, anywhere, anywhere,
            pl.BlockSpec(memory_space=pltpu.SMEM),
            anywhere, anywhere,
        ],
        out_specs=(vmem, vmem),
        scratch_shapes=[
            pltpu.VMEM((2, (FAR + 2) * rows, width), jnp.bfloat16),
            pltpu.VMEM((rows, width), jnp.bfloat16),
            pltpu.VMEM((width, model), jnp.bfloat16),
            pltpu.VMEM((rows, width), jnp.bfloat16),
            pltpu.VMEM((rows, span), jnp.float32),
            pltpu.VMEM((rows, model), jnp.float32),
            pltpu.VMEM((rows, 2 * HEAD_DIM), jnp.bfloat16),
            pltpu.VMEM((rows, width), jnp.bfloat16),
            pltpu.VMEM((rows, width), jnp.bfloat16),
            pltpu.VMEM((rows, width), jnp.bfloat16),
            pltpu.VMEM((rows, 128), jnp.float32),
            pltpu.VMEM((rows, 128), jnp.float32),
            pltpu.SemaphoreType.DMA((2, subs)),
            pltpu.SemaphoreType.DMA((3,)),
            pltpu.SemaphoreType.DMA((9, subs)),
            pltpu.SemaphoreType.DMA((FAR + 2, 2, subs)),
            pltpu.SemaphoreType.DMA((pieces,)),
            pltpu.SemaphoreType.DMA((pieces,)),
            pltpu.SemaphoreType.DMA((2,)),
        ],
        compiler_params=pltpu.CompilerParams(
            collective_id=0, has_side_effects=True, vmem_limit_bytes=62 * 1024 * 1024
        ),
    )(queries, key_rows, value_rows, block_pattern, out_weight, hidden)
    mean_square = jnp.sum(squares, axis=1, keepdims=True) / model
    normed = stream * lax.rsqrt(mean_square + 1e-06) * norm_gain[None, :]
    return (stream.astype(jnp.bfloat16), normed.astype(jnp.bfloat16))


def solution(mesh):
    placed = (
        P("seq", "section"),
        P("seq", "section"),
        P("seq", "section"),
        P("seq", None),
        P("section", None),
        P("seq", "section"),
        P("section"),
    )
    return jax.shard_map(
        shards,
        mesh=mesh,
        in_specs=placed,
        out_specs=(P("seq", "section"), P("seq", "section")),
        check_vma=False,
    )
```

```python
import functools
import math

import jax
import jax.numpy as jnp
from jax import lax
from jax.experimental import pallas as pl
from jax.experimental.pallas import tpu as pltpu
from jax.sharding import PartitionSpec as P

HEAD_DIM = 128
BLOCK = 128
WINDOW_BLOCKS = 8
GROUP = 4
FAR = 5
NEAR = -2
MESH = pl.DeviceIdType.MESH
HIDE = -1e30


def kernel(
    q_hbm, k_hbm, v_hbm, pattern, w_hbm, h_hbm,
    stream_ref, square_ref,
    kv, qbuf, wbuf, hbuf, bias, acc, mixed, mine, outgoing, incoming, square_out, square_in,
    own_sem, load_sem, send_sem, recv_sem, part_send, part_recv, sq_sem,
):
    rows, width = q_hbm.shape
    model = w_hbm.shape[1]
    subs = own_sem.shape[1]
    step_cols = width // subs
    piece = step_cols // 2
    shard = lax.axis_index("seq")
    section = lax.axis_index("section")
    count = lax.axis_size("seq")
    role = lax.rem(shard, GROUP)
    has_prev = shard >= GROUP
    has_next = shard + GROUP < count
    partner = 1 - section

    def base(off):
        return (FAR - off) * rows

    def view(off, k, part, tail):
        start = k * step_cols + (piece if part == 1 else 0)
        size = step_cols if part is None else piece
        cols = pl.ds(pl.multiple_of(start, piece), size)
        first, extent = (base(off) + rows - BLOCK, BLOCK) if tail else (base(off), rows)
        return kv.at[:, pl.ds(first, extent), cols]

    def part_index(part):
        return 1 if part == 1 else 0

    def send(index, k, off, target, to_off, part=None, tail=False):
        return pltpu.make_async_remote_copy(
            src_ref=view(off, k, part, tail),
            dst_ref=view(to_off, k, part, tail),
            send_sem=send_sem.at[index, k],
            recv_sem=recv_sem.at[to_off - NEAR, part_index(part), k],
            device_id={"seq": target},
            device_id_type=MESH,
        )

    def arrive(k, off, part=None, tail=False):
        pltpu.make_async_remote_copy(
            src_ref=view(off, k, part, tail),
            dst_ref=view(off, k, part, tail),
            send_sem=send_sem.at[0, k],
            recv_sem=recv_sem.at[off - NEAR, part_index(part), k],
            device_id={"section": partner},
            device_id_type=MESH,
        ).wait_recv()

    def own_loads(k):
        cols = pl.ds(pl.multiple_of(k * step_cols, step_cols), step_cols)
        return [
            pltpu.make_async_copy(
                source.at[:, cols], kv.at[i, pl.ds(base(0), rows), cols], own_sem.at[i, k]
            )
            for i, source in enumerate((k_hbm, v_hbm))
        ]

    table = [
        (
            [(0, 0, 2, 2, 0, False, None), (1, 0, 1, 1, 0, False, None),
             (2, 0, 2, 2, 1, False, None), (3, 0, 1, 1, 1, False, None),
             (4, 0, 4, 4, None, True, "next")],
            [([(-1, 0, False, None)],
              [(6, -1, 4, 3, 0, False, "next"), (5, -1, 2, 1, 0, False, None)]),
             ([(-2, 0, False, "next")], [(7, -2, 4, 2, 0, False, "next")])],
            [([(2, 0, False, "prev")], [(8, 2, 1, 3, 0, False, "prev")])],
            [(2, 1, False, "prev"), (3, 0, False, "prev"), (4, None, True, "prev"),
             (3, 1, False, "prev"), (1, 0, False, "prev"), (1, 1, False, "prev")],
        ),
        (
            [(0, 0, -1, -1, 0, False, None), (1, 0, 2, 2, 1, False, None),
             (2, 0, 4, 4, 1, False, "next"), (3, 0, 2, 2, 0, False, None),
             (4, 0, 4, 4, 0, True, "next")],
            [([(4, 1, False, "prev")], [(5, 4, -1, 3, 1, False, "prev")]),
             ([(-2, 1, False, "next")], [(8, -2, 4, 2, 1, False, "next")]),
             ([(1, 0, False, None)], [(6, 1, 2, 3, 0, False, None)])],
            [([(2, 0, False, "prev")], [(7, 2, -1, 1, 0, False, "prev")])],
            [(1, 1, False, None), (2, 1, False, "prev"), (4, 0, True, "prev"),
             (3, 0, False, "prev"), (3, 1, False, "prev")],
        ),
        (
            [(2, 0, 4, 4, 1, False, "next"), (0, 0, -2, -2, 0, False, "next"),
             (1, 0, 1, 1, 1, False, None), (3, 0, 1, 1, 0, False, None),
             (4, 0, 4, 4, 0, True, "next")],
            [([(4, 1, False, "prev")], [(5, 4, -2, 2, 1, False, "prev")]),
             ([(-1, 0, False, "next")], [(8, -1, 4, 3, 0, False, "next")]),
             ([(2, 1, False, None)], [(6, 2, 1, 3, 1, False, None)])],
            [([(3, 1, False, "prev")], [(7, 3, -2, 1, 1, False, "prev")])],
            [(2, 0, False, None), (3, 0, False, "prev"), (4, 0, True, "prev"),
             (1, 0, False, None), (1, 1, False, None)],
        ),
        (
            [(0, 0, 4, 4, 0, False, "next"), (2, 0, -2, -2, 1, False, "next"),
             (3, 0, -1, -1, 0, False, "next"), (1, 0, 4, 4, 1, False, "next")],
            [([(4, 0, False, "prev")], [(4, 4, -2, 2, 0, False, "prev")]),
             ([(4, 1, False, "prev")], [(5, 4, -1, 3, 1, False, "prev")]),
             ([(1, 1, False, None)], [(7, 1, 4, 5, 1, False, "next")]),
             ([(2, 1, False, None)], [(6, 2, -1, 1, 1, False, None)])],
            [([(5, 1, False, "prev")], [(8, 5, -2, 3, 1, False, "prev")])],
            [(2, 0, False, None), (1, 0, False, None),
             (3, 0, False, None), (3, 1, False, None)],
        ),
    ]

    def grouped(entries, act):
        for need in (None, "prev", "next"):
            chosen = [e for e in entries if e[-1] == need]
            if not chosen:
                continue
            if need is None:
                for e in chosen:
                    act(e)
            else:
                @pl.when(has_prev if need == "prev" else has_next)
                def _():
                    for e in chosen:
                        act(e)

    def start_sends(entries, k):
        def act(e):
            index, off, step, to_off, part, tail, _ = e
            send(index, k, off, shard + step, to_off, part, tail).start()

        grouped(entries, act)

    def end_sends(entries, k):
        def act(e):
            index, off, step, to_off, part, tail, _ = e
            send(index, k, off, shard + step, to_off, part, tail).wait_send()

        grouped(entries, act)

    def waits(entries, k):
        grouped(entries, lambda e: arrive(k, e[0], e[1], e[2]))

    def by_role(body):
        for r in range(GROUP):
            @pl.when(role == r)
            def _():
                body(table[r])

    def first_sends(k):
        for copy in own_loads(k):
            copy.wait()
        by_role(lambda row: start_sends(row[0], k))

    def relay(which, k):
        def body(row):
            for needed, sends in row[which]:
                waits(needed, k)
                start_sends(sends, k)

        by_role(body)

    q_load = pltpu.make_async_copy(q_hbm, qbuf, load_sem.at[0])
    w_load = pltpu.make_async_copy(w_hbm, wbuf, load_sem.at[1])
    h_load = pltpu.make_async_copy(h_hbm, hbuf, load_sem.at[2])

    for k in range(subs):
        for copy in own_loads(k):
            copy.start()
    q_load.start()
    w_load.start()
    h_load.start()

    barrier = pltpu.get_barrier_semaphore()
    across = jnp.where(lax.rem(role, 2) == 0, shard + 1, shard - 1)
    along = jnp.where(role < 2, shard + 2, shard - 2)
    pl.semaphore_signal(barrier, inc=1, device_id={"seq": across}, device_id_type=MESH)
    pl.semaphore_signal(barrier, inc=1, device_id={"seq": along}, device_id_type=MESH)
    pl.semaphore_signal(barrier, inc=1, device_id={"section": partner}, device_id_type=MESH)

    @pl.when(has_prev)
    def _():
        pl.semaphore_signal(
            barrier, inc=1, device_id={"seq": shard - GROUP}, device_id_type=MESH
        )

    @pl.when(has_next)
    def _():
        pl.semaphore_signal(
            barrier, inc=1, device_id={"seq": shard + GROUP}, device_id_type=MESH
        )

    pl.semaphore_wait(barrier, 3 + has_prev.astype(jnp.int32) + has_next.astype(jnp.int32))

    first_sends(0)

    for off in range(1, GROUP + 1):
        @pl.when(shard < off)
        def _():
            kv[:, pl.ds(base(off), rows), :] = jnp.zeros((2, rows, width), kv.dtype)

    query_place = lax.broadcasted_iota(jnp.int32, (BLOCK, BLOCK), 0)
    key_place = lax.broadcasted_iota(jnp.int32, (BLOCK, BLOCK), 1)
    blocks = rows // BLOCK
    span_blocks = WINDOW_BLOCKS - 1 + blocks
    for i in range(blocks):
        for g in range(span_blocks):
            j = i + WINDOW_BLOCKS - 1 - g
            if j < 0 or j >= WINDOW_BLOCKS:
                value = jnp.full((BLOCK, BLOCK), HIDE, jnp.float32)
            else:
                seen = (pattern[i, j] == 1) & (shard * blocks + i - j >= 0)
                level = jnp.where(seen, 0.0, HIDE).astype(jnp.float32)
                value = jnp.full((BLOCK, BLOCK), level, jnp.float32)
                if j == 0:
                    value = jnp.where(key_place <= query_place, value, HIDE)
            bias[i * BLOCK : (i + 1) * BLOCK, g * BLOCK : (g + 1) * BLOCK] = value
    acc[...] = jnp.zeros(acc.shape, acc.dtype)
    q_load.wait()
    w_load.wait()
    h_load.wait()

    key_first = base(GROUP) + rows - BLOCK
    key_span = span_blocks * BLOCK
    factor = math.log2(math.e) / math.sqrt(HEAD_DIM)
    tile = math.gcd(model, 1024)

    def heads(k):
        by_role(lambda row: waits(row[3], k))
        for n in range(step_cols // HEAD_DIM):
            cols = pl.ds(pl.multiple_of(k * step_cols + n * HEAD_DIM, HEAD_DIM), HEAD_DIM)
            query = qbuf[:, cols]
            keys = kv[0, pl.ds(key_first, key_span), cols]
            values = kv[1, pl.ds(key_first, key_span), cols]
            scores = lax.dot_general(
                query, keys, (((1,), (1,)), ((), ())), preferred_element_type=jnp.float32
            )
            scores = scores + bias[...]
            largest = jnp.max(scores, axis=1, keepdims=True)
            exponent = jnp.exp2((scores - largest) * factor)
            total = jnp.sum(exponent, axis=1, keepdims=True)
            mixture = jnp.dot(
                exponent.astype(jnp.bfloat16), values, preferred_element_type=jnp.float32
            )
            mixed[:, n * HEAD_DIM : (n + 1) * HEAD_DIM] = (mixture / total).astype(jnp.bfloat16)

    def attend(k):
        heads(k)
        depth = pl.ds(pl.multiple_of(k * step_cols, step_cols), step_cols)
        for c in range(0, model, tile):
            acc[:, c : c + tile] += jnp.dot(
                mixed[...], wbuf[depth, c : c + tile], preferred_element_type=jnp.float32
            )

    @pl.loop(0, subs)
    def _(t):
        @pl.when(t + 1 < subs)
        def _():
            first_sends(t + 1)

        relay(1, t)

        @pl.when(t >= 1)
        def _():
            relay(2, t - 1)

        @pl.when(t >= 2)
        def _():
            attend(t - 2)

    attend(subs - 2)
    relay(2, subs - 1)
    heads(subs - 1)

    pieces = part_send.shape[0]
    part_cols = width // pieces

    def part_copy(c):
        cols = pl.ds(c * part_cols, part_cols)
        return pltpu.make_async_remote_copy(
            src_ref=outgoing.at[:, cols],
            dst_ref=incoming.at[:, cols],
            send_sem=part_send.at[c],
            recv_sem=part_recv.at[c],
            device_id={"section": partner},
            device_id_type=MESH,
        )

    last = pl.ds((subs - 1) * step_cols, step_cols)

    def last_sum(start):
        cols = pl.ds(pl.multiple_of(start, part_cols), part_cols)
        return acc[:, cols] + jnp.dot(
            mixed[...], wbuf[last, cols], preferred_element_type=jnp.float32
        )

    for c in range(pieces):
        outgoing[:, c * part_cols : (c + 1) * part_cols] = last_sum(
            partner * width + c * part_cols
        ).astype(outgoing.dtype)
        if c >= 1:
            part_copy(c - 1).start()
    for c in range(pieces):
        cols = slice(c * part_cols, (c + 1) * part_cols)
        mine[:, cols] = last_sum(section * width + c * part_cols).astype(mine.dtype)
        if c == 0:
            part_copy(pieces - 1).start()
    for c in range(pieces):
        part_copy(c).wait_recv()

    strip = 16

    @pl.loop(0, rows // strip)
    def _(i):
        place = pl.ds(pl.multiple_of(i * strip, strip), strip)
        here = mine[place, :].astype(jnp.float32)
        there = incoming[place, :].astype(jnp.float32)
        stream = hbuf[place, :].astype(jnp.float32) + (here + there)
        stream_ref[place, :] = stream
        squares = stream * stream
        lanes = squares[:, 0:128]
        for c in range(128, width, 128):
            lanes = lanes + squares[:, c : c + 128]
        square_out[place, :] = lanes

    square_copy = pltpu.make_async_remote_copy(
        src_ref=square_out,
        dst_ref=square_in,
        send_sem=sq_sem.at[0],
        recv_sem=sq_sem.at[1],
        device_id={"section": partner},
        device_id_type=MESH,
    )
    square_copy.start()

    @pl.loop(0, subs)
    def _(k):
        def body(row):
            end_sends(row[0], k)
            for which in (1, 2):
                for _, sends in row[which]:
                    end_sends(sends, k)

        by_role(body)

    for c in range(pieces):
        part_copy(c).wait_send()
    square_copy.wait()
    square_ref[...] = square_out[...] + square_in[...]


def shards(queries, key_rows, value_rows, block_pattern, out_weight, hidden, norm_gain):
    rows, width = queries.shape
    model = out_weight.shape[1]
    subs = width // (2 * HEAD_DIM)
    pieces = 4
    span = (WINDOW_BLOCKS - 1) * BLOCK + rows
    anywhere = pl.BlockSpec(memory_space=pl.ANY)
    vmem = pl.BlockSpec(memory_space=pltpu.VMEM)
    stream, squares = pl.pallas_call(
        kernel,
        out_shape=(
            jax.ShapeDtypeStruct((rows, width), jnp.float32),
            jax.ShapeDtypeStruct((rows, 128), jnp.float32),
        ),
        in_specs=[
            anywhere, anywhere, anywhere,
            pl.BlockSpec(memory_space=pltpu.SMEM),
            anywhere, anywhere,
        ],
        out_specs=(vmem, vmem),
        scratch_shapes=[
            pltpu.VMEM((2, (FAR + 1 - NEAR) * rows, width), jnp.bfloat16),
            pltpu.VMEM((rows, width), jnp.bfloat16),
            pltpu.VMEM((width, model), jnp.bfloat16),
            pltpu.VMEM((rows, width), jnp.bfloat16),
            pltpu.VMEM((rows, span), jnp.float32),
            pltpu.VMEM((rows, model), jnp.float32),
            pltpu.VMEM((rows, 2 * HEAD_DIM), jnp.bfloat16),
            pltpu.VMEM((rows, width), jnp.bfloat16),
            pltpu.VMEM((rows, width), jnp.bfloat16),
            pltpu.VMEM((rows, width), jnp.bfloat16),
            pltpu.VMEM((rows, 128), jnp.float32),
            pltpu.VMEM((rows, 128), jnp.float32),
            pltpu.SemaphoreType.DMA((2, subs)),
            pltpu.SemaphoreType.DMA((3,)),
            pltpu.SemaphoreType.DMA((9, subs)),
            pltpu.SemaphoreType.DMA((FAR + 1 - NEAR, 2, subs)),
            pltpu.SemaphoreType.DMA((pieces,)),
            pltpu.SemaphoreType.DMA((pieces,)),
            pltpu.SemaphoreType.DMA((2,)),
        ],
        compiler_params=pltpu.CompilerParams(
            collective_id=0, has_side_effects=True, vmem_limit_bytes=62 * 1024 * 1024
        ),
    )(queries, key_rows, value_rows, block_pattern, out_weight, hidden)
    mean_square = jnp.sum(squares, axis=1, keepdims=True) / model
    normed = stream * lax.rsqrt(mean_square + 1e-06) * norm_gain[None, :]
    return (stream.astype(jnp.bfloat16), normed.astype(jnp.bfloat16))


def solution(mesh):
    placed = (
        P("seq", "section"),
        P("seq", "section"),
        P("seq", "section"),
        P("seq", None),
        P("section", None),
        P("seq", "section"),
        P("section"),
    )
    return jax.shard_map(
        shards,
        mesh=mesh,
        in_specs=placed,
        out_specs=(P("seq", "section"), P("seq", "section")),
        check_vma=False,
    )
```

```python
import functools
import math

import jax
import jax.numpy as jnp
from jax import lax
from jax.experimental import pallas as pl
from jax.experimental.pallas import tpu as pltpu
from jax.sharding import PartitionSpec as P

HEAD_DIM = 128
BLOCK = 128
WINDOW_BLOCKS = 8
GROUP = 4
FAR = 5
NEAR = -2
MESH = pl.DeviceIdType.MESH
HIDE = -1e30


def kernel(
    q_hbm, k_hbm, v_hbm, pattern, w_hbm, h_hbm,
    stream_ref, square_ref,
    kv, qbuf, wbuf, hbuf, bias, acc, mixed, mine, outgoing, incoming, square_out, square_in,
    own_sem, load_sem, send_sem, recv_sem, part_send, part_recv, sq_sem,
):
    rows, width = q_hbm.shape
    model = w_hbm.shape[1]
    subs = own_sem.shape[1]
    step_cols = width // subs
    piece = step_cols // 2
    shard = lax.axis_index("seq")
    section = lax.axis_index("section")
    count = lax.axis_size("seq")
    role = lax.rem(shard, GROUP)
    has_prev = shard >= GROUP
    has_next = shard + GROUP < count
    partner = 1 - section

    def base(off):
        return (FAR - off) * rows

    def view(off, k, part, tail):
        start = k * step_cols + (piece if part == 1 else 0)
        size = step_cols if part is None else piece
        cols = pl.ds(pl.multiple_of(start, piece), size)
        first, extent = (base(off) + rows - BLOCK, BLOCK) if tail else (base(off), rows)
        return kv.at[:, pl.ds(first, extent), cols]

    def part_index(part):
        return 1 if part == 1 else 0

    def send(index, k, off, target, to_off, part=None, tail=False):
        return pltpu.make_async_remote_copy(
            src_ref=view(off, k, part, tail),
            dst_ref=view(to_off, k, part, tail),
            send_sem=send_sem.at[index, k],
            recv_sem=recv_sem.at[to_off - NEAR, part_index(part), k],
            device_id={"seq": target},
            device_id_type=MESH,
        )

    def arrive(k, off, part=None, tail=False):
        pltpu.make_async_remote_copy(
            src_ref=view(off, k, part, tail),
            dst_ref=view(off, k, part, tail),
            send_sem=send_sem.at[0, k],
            recv_sem=recv_sem.at[off - NEAR, part_index(part), k],
            device_id={"section": partner},
            device_id_type=MESH,
        ).wait_recv()

    def own_loads(k):
        cols = pl.ds(pl.multiple_of(k * step_cols, step_cols), step_cols)
        return [
            pltpu.make_async_copy(
                source.at[:, cols], kv.at[i, pl.ds(base(0), rows), cols], own_sem.at[i, k]
            )
            for i, source in enumerate((k_hbm, v_hbm))
        ]

    table = [
        (
            [(0, 0, 2, 2, 0, False, None), (1, 0, 1, 1, 0, False, None),
             (2, 0, 2, 2, 1, False, None), (3, 0, 1, 1, 1, False, None),
             (4, 0, 4, 4, None, True, "next")],
            [([(-1, 0, False, None)],
              [(6, -1, 4, 3, 0, False, "next"), (5, -1, 2, 1, 0, False, None)]),
             ([(-2, 0, False, "next")], [(7, -2, 4, 2, 0, False, "next")])],
            [([(2, 0, False, "prev")], [(8, 2, 1, 3, 0, False, "prev")])],
            [(2, 1, False, "prev"), (3, 0, False, "prev"), (4, None, True, "prev"),
             (3, 1, False, "prev"), (1, 0, False, "prev"), (1, 1, False, "prev")],
        ),
        (
            [(0, 0, -1, -1, 0, False, None), (1, 0, 2, 2, 1, False, None),
             (2, 0, 4, 4, 1, False, "next"), (3, 0, 2, 2, 0, False, None),
             (4, 0, 4, 4, 0, True, "next")],
            [([(4, 1, False, "prev")], [(5, 4, -1, 3, 1, False, "prev")]),
             ([(-2, 1, False, "next")], [(8, -2, 4, 2, 1, False, "next")]),
             ([(1, 0, False, None)], [(6, 1, 2, 3, 0, False, None)])],
            [([(2, 0, False, "prev")], [(7, 2, -1, 1, 0, False, "prev")])],
            [(1, 1, False, None), (2, 1, False, "prev"), (4, 0, True, "prev"),
             (3, 0, False, "prev"), (3, 1, False, "prev")],
        ),
        (
            [(2, 0, 4, 4, 1, False, "next"), (0, 0, -2, -2, 0, False, "next"),
             (1, 0, 1, 1, 1, False, None), (3, 0, 1, 1, 0, False, None),
             (4, 0, 4, 4, 0, True, "next")],
            [([(4, 1, False, "prev")], [(5, 4, -2, 2, 1, False, "prev")]),
             ([(-1, 0, False, "next")], [(8, -1, 4, 3, 0, False, "next")]),
             ([(2, 1, False, None)], [(6, 2, 1, 3, 1, False, None)])],
            [([(3, 1, False, "prev")], [(7, 3, -2, 1, 1, False, "prev")])],
            [(2, 0, False, None), (3, 0, False, "prev"), (4, 0, True, "prev"),
             (1, 0, False, None), (1, 1, False, None)],
        ),
        (
            [(0, 0, 4, 4, 0, False, "next"), (2, 0, -2, -2, 1, False, "next"),
             (3, 0, -1, -1, 0, False, "next"), (1, 0, 4, 4, 1, False, "next")],
            [([(4, 0, False, "prev")], [(4, 4, -2, 2, 0, False, "prev")]),
             ([(4, 1, False, "prev")], [(5, 4, -1, 3, 1, False, "prev")]),
             ([(1, 1, False, None)], [(7, 1, 4, 5, 1, False, "next")]),
             ([(2, 1, False, None)], [(6, 2, -1, 1, 1, False, None)])],
            [([(5, 1, False, "prev")], [(8, 5, -2, 3, 1, False, "prev")])],
            [(2, 0, False, None), (1, 0, False, None),
             (3, 0, False, None), (3, 1, False, None)],
        ),
    ]

    def grouped(entries, act):
        for need in (None, "prev", "next"):
            chosen = [e for e in entries if e[-1] == need]
            if not chosen:
                continue
            if need is None:
                for e in chosen:
                    act(e)
            else:
                @pl.when(has_prev if need == "prev" else has_next)
                def _():
                    for e in chosen:
                        act(e)

    def start_sends(entries, k):
        def act(e):
            index, off, step, to_off, part, tail, _ = e
            send(index, k, off, shard + step, to_off, part, tail).start()

        grouped(entries, act)

    def end_sends(entries, k):
        def act(e):
            index, off, step, to_off, part, tail, _ = e
            send(index, k, off, shard + step, to_off, part, tail).wait_send()

        grouped(entries, act)

    def waits(entries, k):
        grouped(entries, lambda e: arrive(k, e[0], e[1], e[2]))

    def by_role(body):
        for r in range(GROUP):
            @pl.when(role == r)
            def _():
                body(table[r])

    def first_sends(k):
        for copy in own_loads(k):
            copy.wait()
        by_role(lambda row: start_sends(row[0], k))

    def relay(which, k):
        def body(row):
            for needed, sends in row[which]:
                waits(needed, k)
                start_sends(sends, k)

        by_role(body)

    q_load = pltpu.make_async_copy(q_hbm, qbuf, load_sem.at[0])
    w_load = pltpu.make_async_copy(w_hbm, wbuf, load_sem.at[1])
    h_load = pltpu.make_async_copy(h_hbm, hbuf, load_sem.at[2])

    for k in range(subs):
        for copy in own_loads(k):
            copy.start()
    q_load.start()
    w_load.start()
    h_load.start()

    barrier = pltpu.get_barrier_semaphore()
    across = jnp.where(lax.rem(role, 2) == 0, shard + 1, shard - 1)
    along = jnp.where(role < 2, shard + 2, shard - 2)
    pl.semaphore_signal(barrier, inc=1, device_id={"seq": across}, device_id_type=MESH)
    pl.semaphore_signal(barrier, inc=1, device_id={"seq": along}, device_id_type=MESH)
    pl.semaphore_signal(barrier, inc=1, device_id={"section": partner}, device_id_type=MESH)

    @pl.when(has_prev)
    def _():
        pl.semaphore_signal(
            barrier, inc=1, device_id={"seq": shard - GROUP}, device_id_type=MESH
        )

    @pl.when(has_next)
    def _():
        pl.semaphore_signal(
            barrier, inc=1, device_id={"seq": shard + GROUP}, device_id_type=MESH
        )

    pl.semaphore_wait(barrier, 3 + has_prev.astype(jnp.int32) + has_next.astype(jnp.int32))

    first_sends(0)

    for off in range(1, GROUP + 1):
        @pl.when(shard < off)
        def _():
            kv[:, pl.ds(base(off), rows), :] = jnp.zeros((2, rows, width), kv.dtype)

    query_place = lax.broadcasted_iota(jnp.int32, (BLOCK, BLOCK), 0)
    key_place = lax.broadcasted_iota(jnp.int32, (BLOCK, BLOCK), 1)
    blocks = rows // BLOCK
    span_blocks = WINDOW_BLOCKS - 1 + blocks
    for i in range(blocks):
        for g in range(span_blocks):
            j = i + WINDOW_BLOCKS - 1 - g
            if j < 0 or j >= WINDOW_BLOCKS:
                value = jnp.full((BLOCK, BLOCK), HIDE, jnp.float32)
            else:
                seen = (pattern[i, j] == 1) & (shard * blocks + i - j >= 0)
                level = jnp.where(seen, 0.0, HIDE).astype(jnp.float32)
                value = jnp.full((BLOCK, BLOCK), level, jnp.float32)
                if j == 0:
                    value = jnp.where(key_place <= query_place, value, HIDE)
            bias[i * BLOCK : (i + 1) * BLOCK, g * BLOCK : (g + 1) * BLOCK] = value
    acc[...] = jnp.zeros(acc.shape, acc.dtype)
    q_load.wait()
    w_load.wait()
    h_load.wait()

    key_first = base(GROUP) + rows - BLOCK
    key_span = span_blocks * BLOCK
    factor = math.log2(math.e) / math.sqrt(HEAD_DIM)
    tile = math.gcd(model, 1024)

    def heads(k):
        by_role(lambda row: waits(row[3], k))
        for n in range(step_cols // HEAD_DIM):
            cols = pl.ds(pl.multiple_of(k * step_cols + n * HEAD_DIM, HEAD_DIM), HEAD_DIM)
            query = qbuf[:, cols]
            keys = kv[0, pl.ds(key_first, key_span), cols]
            values = kv[1, pl.ds(key_first, key_span), cols]
            scores = lax.dot_general(
                query, keys, (((1,), (1,)), ((), ())), preferred_element_type=jnp.float32
            )
            scores = scores + bias[...]
            largest = jnp.max(scores, axis=1, keepdims=True)
            exponent = jnp.exp2((scores - largest) * factor)
            total = jnp.sum(exponent, axis=1, keepdims=True)
            mixture = jnp.dot(
                exponent.astype(jnp.bfloat16), values, preferred_element_type=jnp.float32
            )
            mixed[:, n * HEAD_DIM : (n + 1) * HEAD_DIM] = (mixture / total).astype(jnp.bfloat16)

    def attend(k):
        heads(k)
        depth = pl.ds(pl.multiple_of(k * step_cols, step_cols), step_cols)
        for c in range(0, model, tile):
            acc[:, c : c + tile] += jnp.dot(
                mixed[...], wbuf[depth, c : c + tile], preferred_element_type=jnp.float32
            )

    @pl.loop(0, subs)
    def _(t):
        @pl.when(t + 1 < subs)
        def _():
            first_sends(t + 1)

        relay(1, t)

        @pl.when(t >= 1)
        def _():
            relay(2, t - 1)

        @pl.when(t >= 3)
        def _():
            attend(t - 3)

    attend(subs - 3)
    relay(2, subs - 1)
    attend(subs - 2)
    heads(subs - 1)

    pieces = part_send.shape[0]
    part_cols = width // pieces

    def part_copy(c):
        cols = pl.ds(c * part_cols, part_cols)
        return pltpu.make_async_remote_copy(
            src_ref=outgoing.at[:, cols],
            dst_ref=incoming.at[:, cols],
            send_sem=part_send.at[c],
            recv_sem=part_recv.at[c],
            device_id={"section": partner},
            device_id_type=MESH,
        )

    last = pl.ds((subs - 1) * step_cols, step_cols)

    def last_sum(start):
        cols = pl.ds(pl.multiple_of(start, part_cols), part_cols)
        return acc[:, cols] + jnp.dot(
            mixed[...], wbuf[last, cols], preferred_element_type=jnp.float32
        )

    for c in range(pieces):
        outgoing[:, c * part_cols : (c + 1) * part_cols] = last_sum(
            partner * width + c * part_cols
        ).astype(outgoing.dtype)
        if c >= 1:
            part_copy(c - 1).start()
    for c in range(pieces):
        cols = slice(c * part_cols, (c + 1) * part_cols)
        mine[:, cols] = last_sum(section * width + c * part_cols).astype(mine.dtype)
        if c == 0:
            part_copy(pieces - 1).start()
    for c in range(pieces):
        part_copy(c).wait_recv()

    strip = 16

    @pl.loop(0, rows // strip)
    def _(i):
        place = pl.ds(pl.multiple_of(i * strip, strip), strip)
        here = mine[place, :].astype(jnp.float32)
        there = incoming[place, :].astype(jnp.float32)
        stream = hbuf[place, :].astype(jnp.float32) + (here + there)
        stream_ref[place, :] = stream
        squares = stream * stream
        lanes = squares[:, 0:128]
        for c in range(128, width, 128):
            lanes = lanes + squares[:, c : c + 128]
        square_out[place, :] = lanes

    square_copy = pltpu.make_async_remote_copy(
        src_ref=square_out,
        dst_ref=square_in,
        send_sem=sq_sem.at[0],
        recv_sem=sq_sem.at[1],
        device_id={"section": partner},
        device_id_type=MESH,
    )
    square_copy.start()

    @pl.loop(0, subs)
    def _(k):
        def body(row):
            end_sends(row[0], k)
            for which in (1, 2):
                for _, sends in row[which]:
                    end_sends(sends, k)

        by_role(body)

    for c in range(pieces):
        part_copy(c).wait_send()
    square_copy.wait()
    square_ref[...] = square_out[...] + square_in[...]


def shards(queries, key_rows, value_rows, block_pattern, out_weight, hidden, norm_gain):
    rows, width = queries.shape
    model = out_weight.shape[1]
    subs = width // (2 * HEAD_DIM)
    pieces = 4
    span = (WINDOW_BLOCKS - 1) * BLOCK + rows
    anywhere = pl.BlockSpec(memory_space=pl.ANY)
    vmem = pl.BlockSpec(memory_space=pltpu.VMEM)
    stream, squares = pl.pallas_call(
        kernel,
        out_shape=(
            jax.ShapeDtypeStruct((rows, width), jnp.float32),
            jax.ShapeDtypeStruct((rows, 128), jnp.float32),
        ),
        in_specs=[
            anywhere, anywhere, anywhere,
            pl.BlockSpec(memory_space=pltpu.SMEM),
            anywhere, anywhere,
        ],
        out_specs=(vmem, vmem),
        scratch_shapes=[
            pltpu.VMEM((2, (FAR + 1 - NEAR) * rows, width), jnp.bfloat16),
            pltpu.VMEM((rows, width), jnp.bfloat16),
            pltpu.VMEM((width, model), jnp.bfloat16),
            pltpu.VMEM((rows, width), jnp.bfloat16),
            pltpu.VMEM((rows, span), jnp.float32),
            pltpu.VMEM((rows, model), jnp.float32),
            pltpu.VMEM((rows, 2 * HEAD_DIM), jnp.bfloat16),
            pltpu.VMEM((rows, width), jnp.bfloat16),
            pltpu.VMEM((rows, width), jnp.bfloat16),
            pltpu.VMEM((rows, width), jnp.bfloat16),
            pltpu.VMEM((rows, 128), jnp.float32),
            pltpu.VMEM((rows, 128), jnp.float32),
            pltpu.SemaphoreType.DMA((2, subs)),
            pltpu.SemaphoreType.DMA((3,)),
            pltpu.SemaphoreType.DMA((9, subs)),
            pltpu.SemaphoreType.DMA((FAR + 1 - NEAR, 2, subs)),
            pltpu.SemaphoreType.DMA((pieces,)),
            pltpu.SemaphoreType.DMA((pieces,)),
            pltpu.SemaphoreType.DMA((2,)),
        ],
        compiler_params=pltpu.CompilerParams(
            collective_id=0, has_side_effects=True, vmem_limit_bytes=62 * 1024 * 1024
        ),
    )(queries, key_rows, value_rows, block_pattern, out_weight, hidden)
    mean_square = jnp.sum(squares, axis=1, keepdims=True) / model
    normed = stream * lax.rsqrt(mean_square + 1e-06) * norm_gain[None, :]
    return (stream.astype(jnp.bfloat16), normed.astype(jnp.bfloat16))


def solution(mesh):
    placed = (
        P("seq", "section"),
        P("seq", "section"),
        P("seq", "section"),
        P("seq", None),
        P("section", None),
        P("seq", "section"),
        P("section"),
    )
    return jax.shard_map(
        shards,
        mesh=mesh,
        in_specs=placed,
        out_specs=(P("seq", "section"), P("seq", "section")),
        check_vma=False,
    )
```
